32 devices in a mesh: cores: 4 (over z), mode: 8 (over y, x, core).
Axes of the slice: x: 2, y: 2, z: 4, core: 2. Of those that a mesh axis runs over, the one named last changes fastest.
Arguments:
- summand_cores: bfloat16 [4, 3, 16, 16, 256], P('cores'), may hold values from -1.5 to 1.5
- sketch_cores: bfloat16 [4, 640, 10240], P('cores', None, 'mode'), may hold values from -0.0625 to 0.0625
- arrivals: bfloat16 [4, 256, 640], P('cores', 'mode'), may hold values from -6 to 6
- entering: bfloat16 [2, 256, 640], P(None, 'mode'), may hold values from -6 to 6
Outputs:
- interfaces: bfloat16 [4, 3, 256, 640], P('cores', None, 'mode')
The draws below stay inside these ranges and needn't reach their ends.
All inputs are finite; a program needn't handle non-finite values.
Results may differ from the reference program's by a relative error of at most 0.024.
Values may be sent and summed in bfloat16 or wider, within the bound.
No kernel may reach another device: no remote copies, remote signals or barrier semaphores. Data moves between devices by JAX's collectives and lax.ppermute only.
A program may use at most 64 MiB of HBM per device.

```python
import jax
import jax.numpy as jnp
from jax import lax

R = 640
MODE = 16
RS = 16
SUMS = 16
TURNS = 3
ROWS = 256
CORES = 4
N_MODE = 8


def steps_of(stream_key, dims, shards, low, largest):
    def one(dim, blocks):
        draws = jax.random.uniform(jax.random.fold_in(jax.random.fold_in(stream_key, 6), dim), (blocks,), jnp.float32, low / len(shards), largest / len(shards))
        return jnp.repeat(jnp.exp(draws), dims[dim] // blocks).reshape((-1,) + (1,) * (len(dims) - dim - 1))

    gain = one(*shards[0])
    for cut in shards[1:]:
        gain = gain * one(*cut)
    return gain


def gaussian(rng, extent, scale, limit, cuts=(), held_as=jnp.bfloat16):
    values = scale * jax.random.normal(rng, extent, jnp.float32)
    if cuts:
        values = values * steps_of(rng, extent, cuts, -0.22, 0.18)
    return jnp.clip(values, -limit, limit).astype(held_as)


def setup_inputs(seed: int = 0) -> dict:
    key_of = jax.random.split(jax.random.key(seed), 5)
    summand_cores = gaussian(key_of[0], (CORES, TURNS, MODE, RS, ROWS), RS ** -0.5, 1.5, ((0, 4),))
    sketch_cores = gaussian(key_of[1], (CORES, R, MODE * R), (MODE * R) ** -0.5, 0.0625, ((0, 4), (2, 8)))
    arrivals = gaussian(key_of[2], (CORES, ROWS, R), 1.0, 6.0, ((0, 4), (1, 8)))
    entering = gaussian(key_of[3], (TURNS - 1, ROWS, R), 1.0, 6.0, ((1, 8),))
    return dict(summand_cores=summand_cores, sketch_cores=sketch_cores, arrivals=arrivals, entering=entering)


def one_core(args):
    xcore, ycore, inter = args
    xs = xcore.astype(jnp.float32).reshape(MODE, RS, SUMS, RS)
    ws = inter.astype(jnp.float32).reshape(SUMS, RS, R)
    amat = jnp.einsum("ibsa,sbd->said", xs, ws).reshape(ROWS, MODE * R).astype(jnp.bfloat16)
    width = MODE * R // N_MODE
    ablocks = amat.astype(jnp.float32).reshape(ROWS, N_MODE, width)
    yblocks = ycore.astype(jnp.float32).reshape(R, N_MODE, width)
    parts = jnp.einsum("rjk,cjk->jrc", ablocks, yblocks).astype(jnp.bfloat16)
    parts = lax.optimization_barrier(parts)
    return jnp.sum(parts.astype(jnp.float32), axis=0).astype(jnp.bfloat16)


def reference(summand_cores, sketch_cores, arrivals, entering):
    current = arrivals
    results = []
    for turn in range(TURNS):
        made = lax.map(one_core, (summand_cores[:, turn], sketch_cores, current))
        results.append(made)
        if turn + 1 < TURNS:
            current = jnp.concatenate([made[1:], entering[turn][None]], axis=0)
    return jnp.stack(results, axis=1)
```

```python
import functools

import jax
import jax.numpy as jnp
from jax import lax
from jax.experimental import pallas as pl
from jax.experimental.pallas import tpu as pltpu
from jax.sharding import PartitionSpec as P

RS = 16
LANES = 128


def passed_along(block, axis, distance):
    devices = range(lax.axis_size(axis))
    route = [(i - distance, i) for i in devices if i - distance in devices]
    return lax.ppermute(block, axis, route)


def contract_cols(xturn, wpart, position, width, rank):
    rows = xturn.shape[-1]
    modes_here = max(width // rank, 1)
    cols_here = min(width, rank)
    first_mode = position * width // rank
    xpart = lax.dynamic_slice_in_dim(xturn, first_mode, modes_here, 0)
    xpart = xpart.reshape(modes_here, RS, rows // RS, RS)
    wsplit = wpart.reshape(rows // RS, RS, cols_here)
    amat = jnp.einsum("ibsa,sbd->said", xpart, wsplit, preferred_element_type=jnp.float32)
    return amat.reshape(rows, modes_here * cols_here).astype(jnp.bfloat16)


def contract_left(xturn, whole, position, width):
    rank = whole.shape[1]
    cols_here = min(width, rank)
    first_col = position * width % rank
    wpart = lax.dynamic_slice_in_dim(whole, first_col, cols_here, 1)
    return contract_cols(xturn, wpart, position, width, rank)


def per_device_general(summand_cores, sketch_cores, arrivals, entering):
    ycore = sketch_cores[0]
    width = ycore.shape[1]
    turns = summand_cores.shape[1]
    position = lax.axis_index("mode")
    is_last = lax.axis_index("cores") == lax.axis_size("cores") - 1
    results = []
    current = arrivals[0]
    for turn in range(turns):
        whole = lax.all_gather(current, "mode", axis=0, tiled=True)
        amat = contract_left(summand_cores[0, turn], whole, position, width)
        mine = lax.psum_scatter(
            lax.dot_general(
                amat, ycore, (((1,), (1,)), ((), ())), preferred_element_type=jnp.float32
            ).astype(jnp.bfloat16),
            "mode",
            scatter_dimension=0,
            tiled=True,
        )
        results.append(mine)
        if turn + 1 < turns:
            passed = passed_along(mine, "cores", -1)
            current = jnp.where(is_last, entering[turn], passed)
    return jnp.stack(results, axis=0)[None]


def turn_kernel(peers, modes_here, x_ref, *refs):
    w_refs, (yown_ref, yother_ref), out_refs = refs[:peers], refs[peers:peers + 2], refs[peers + 2:]
    rows_dev, rank = w_refs[0].shape
    rows = peers * rows_dev
    all_rows = x_ref.shape[-1]
    me = lax.axis_index("mode")

    place = lax.broadcasted_iota(jnp.int32, (rows, all_rows), 0)
    column = lax.broadcasted_iota(jnp.int32, (rows, all_rows), 1)
    owner = me ^ (2 * (place // rows_dev))
    pick = (column == owner * rows_dev + place % rows_dev).astype(jnp.float32).astype(jnp.bfloat16)

    modes = [me * modes_here + m for m in range(modes_here)]
    modes += [(me ^ 1) * modes_here + m for m in range(modes_here)]
    spread = jnp.concatenate([x_ref[i] for i in modes for _ in range(rows // RS)], axis=0)
    chosen = lax.dot_general(pick, spread, (((1,), (1,)), ((), ())), preferred_element_type=jnp.float32)
    left = lax.broadcasted_iota(jnp.int32, (rows, rows), 0) // RS
    right = lax.broadcasted_iota(jnp.int32, (rows, rows), 1) // RS
    same = left == right

    whole = jnp.concatenate([w[...] for w in w_refs], axis=0)
    total = jnp.zeros((rows, rank), jnp.float32)
    for n in range(len(modes)):
        y_ref = yown_ref if n < modes_here else yother_ref
        m = n % modes_here
        diag = jnp.where(same, chosen[:, n * rows:(n + 1) * rows], 0.0).astype(jnp.bfloat16)
        amat = jnp.dot(diag, whole, preferred_element_type=jnp.float32).astype(jnp.bfloat16)
        total += lax.dot_general(
            amat,
            y_ref[:, m * rank:(m + 1) * rank],
            (((1,), (1,)), ((), ())),
            preferred_element_type=jnp.float32,
        )
    for d, out in enumerate(out_refs):
        out[...] = total[d * rows_dev:(d + 1) * rows_dev].astype(out.dtype)


def make_turn(peers, modes_here, xturn, wparts, yown, yother):
    rows_dev, rank = wparts[0].shape
    rows = peers * rows_dev
    flops = 2 * rows * 2 * modes_here * rank * (rank + rows)
    moved = 2 * (yown.size + yother.size + xturn.size + 2 * rows * rank)
    return pl.pallas_call(
        functools.partial(turn_kernel, peers, modes_here),
        out_shape=[jax.ShapeDtypeStruct((rows_dev, rank), jnp.bfloat16)] * peers,
        in_specs=[pl.BlockSpec(memory_space=pltpu.VMEM)] * (peers + 3),
        out_specs=[pl.BlockSpec(memory_space=pltpu.VMEM)] * peers,
        compiler_params=pltpu.CompilerParams(vmem_limit_bytes=16 << 20),
        cost_estimate=pl.CostEstimate(flops=flops, bytes_accessed=moved, transcendentals=0),
    )(xturn, *wparts, yown, yother)


def per_device_paired(summand_cores, sketch_cores, arrivals, entering):
    yown = sketch_cores[0]
    width = yown.shape[1]
    turns = summand_cores.shape[1]
    devices = lax.axis_size("mode")
    peers = devices // 2
    cores = lax.axis_size("cores")
    rank = arrivals.shape[-1]
    modes_here = width // rank
    is_last = lax.axis_index("cores") == cores - 1

    def swap(block, bits):
        return lax.ppermute(block, "mode", [(i, i ^ bits) for i in range(devices)])

    def shift(block):
        return lax.ppermute(block, "cores", [(i, (i - 1) % cores) for i in range(cores)])

    yother = swap(yown, 1)
    results = []
    current = arrivals[0]
    for turn in range(turns):
        wparts = [current] + [swap(current, 2 * d) for d in range(1, peers)]
        parts = make_turn(peers, modes_here, summand_cores[0, turn], wparts, yown, yother)
        arrived = [parts[0]] + [swap(parts[d], 2 * d) for d in range(1, peers)]
        mine = sum(p.astype(jnp.float32) for p in arrived).astype(jnp.bfloat16)
        results.append(mine)
        if turn + 1 < turns:
            current = jnp.where(is_last, entering[turn], shift(mine))
    return jnp.stack(results, axis=0)[None]


def pairs_fit(mesh, summand_cores, sketch_cores, arrivals):
    devices = mesh.shape["mode"]
    rank = arrivals.shape[-1]
    width = sketch_cores.shape[-1] // devices
    rows_dev = arrivals.shape[1] // devices
    power_of_two = devices >= 4 and devices & (devices - 1) == 0
    return power_of_two and width % rank == 0 and rows_dev % RS == 0 and rank % LANES == 0


def solution(mesh):
    in_specs = (
        P("cores", None, None, None, None),
        P("cores", None, "mode"),
        P("cores", "mode", None),
        P(None, "mode", None),
    )
    out_specs = P("cores", None, "mode", None)

    def program(summand_cores, sketch_cores, arrivals, entering):
        fits = pairs_fit(mesh, summand_cores, sketch_cores, arrivals)
        body = per_device_paired if fits else per_device_general
        return jax.shard_map(
            body, mesh=mesh, in_specs=in_specs, out_specs=out_specs, check_vma=False
        )(summand_cores, sketch_cores, arrivals, entering)

    return program
```
